32 devices in a mesh: group: 4 (over y, x), space: 8 (over z, core).
Axes of the slice: x: 2, y: 2, z: 4, core: 2. Of those that a mesh axis runs over, the one named last changes fastest.
Arguments:
- vectors: bfloat16 [128, 2, 3, 4096], P('group', None, None, 'space'), may hold values from -3 to 3
- momentum: int32 [3], replicated, may hold values from -3 to 3
- assignment: int32 [128], replicated, may hold values from 0 to 127, each once
Outputs:
- elementals: float32 [128, 2, 128, 128], P('space', None, 'group')
The draws below stay inside these ranges and needn't reach their ends.
Inputs may be any that keep to these rules, and one draw needn't show every extreme that they name: `assignment`: each eigenvector is named by exactly one slot.
All inputs are finite; a program needn't handle non-finite values.
Results may differ from the reference program's by a relative error of at most 0.0029.
Values may be sent and summed in bfloat16 or wider, within the bound.
A program may use at most 128 MiB of HBM per device.

```python
import math
import jax
import jax.numpy as jnp
from jax import lax

N = 128
L = 64
SITES = 4096


def levels(key, extent, split, low, high):
    gain = 1.0
    for dim, shards_of in split:
        heights = jax.random.uniform(jax.random.fold_in(jax.random.fold_in(key, 6), dim), (shards_of,), jnp.float32, low / len(split), high / len(split))
        gain = gain * jnp.repeat(jnp.exp(heights), extent[dim] // shards_of).reshape((-1,) + (1,) * (len(extent) - 1 - dim))
    return gain


def normal_values(rng, dims, scale, bound, split=(), kind=jnp.bfloat16):
    loudness = levels(rng, dims, split, -0.22, 0.18) if split else 1.0
    drawn = jax.random.normal(rng, dims, jnp.float32) * scale * loudness
    return jnp.minimum(jnp.maximum(drawn, -bound), bound).astype(kind)


def setup_inputs(seed: int = 0) -> dict:
    arg_keys = jax.random.split(jax.random.key(seed), 4)
    vectors = normal_values(arg_keys[0], (N, 2, 3, SITES), 0.5, 3.0, ((0, 4), (3, 8)))
    momentum = jax.random.randint(arg_keys[1], (3,), -3, 4).astype(jnp.int32)
    assignment = jax.random.permutation(arg_keys[2], N).astype(jnp.int32)
    return dict(vectors=vectors, momentum=momentum, assignment=assignment)


def complex_product(left_re, left_im, right_re, right_im):
    return (left_re * right_re - left_im * right_im, left_re * right_im + left_im * right_re)

def weighted_slot(vec32, slot_vec, cosine, sine):
    crosses_re = []
    crosses_im = []
    for colour in range(3):
        second = (colour + 1) % 3
        third = (colour + 2) % 3
        one_re, one_im = complex_product(vec32[:, 0, second], vec32[:, 1, second], slot_vec[0, third], slot_vec[1, third])
        two_re, two_im = complex_product(vec32[:, 0, third], vec32[:, 1, third], slot_vec[0, second], slot_vec[1, second])
        cross_re = one_re - two_re
        cross_im = one_im - two_im
        crosses_re.append(cross_re * cosine - cross_im * sine)
        crosses_im.append(cross_re * sine + cross_im * cosine)
    stacked = jnp.stack([jnp.stack(crosses_re, axis=1), jnp.stack(crosses_im, axis=1)], axis=1)
    return stacked.astype(jnp.bfloat16)

def reference(vectors, momentum, assignment):
    sites = jnp.arange(SITES, dtype=jnp.int32)
    coord_x = sites % L
    coord_y = sites // L % L
    coord_z = sites // (L * L)
    phase_index = jnp.mod(momentum[0] * coord_x + momentum[1] * coord_y + momentum[2] * coord_z, L).astype(jnp.int32)
    angle = phase_index.astype(jnp.float32) * jnp.float32(2.0 * math.pi / L)
    cosine = jnp.cos(angle)
    sine = jnp.sin(angle)
    vec32 = vectors.astype(jnp.float32)
    flat_left = vec32.reshape(N, 2, 3 * SITES)

    def one_slot(index):
        slot_vec = vec32[index]
        weighted = weighted_slot(vec32, slot_vec, cosine, sine).astype(jnp.float32).reshape(N, 2, 3 * SITES)
        products = jnp.einsum('ipx,jqx->ipqj', flat_left, weighted)
        real_part = products[:, 0, 0] - products[:, 1, 1]
        imag_part = products[:, 0, 1] + products[:, 1, 0]
        return jnp.stack([real_part, imag_part], axis=1)
    slots = lax.map(one_slot, assignment)
    scale = 1.0 / math.sqrt(SITES)
    return jnp.transpose(slots, (1, 2, 0, 3)) * jnp.float32(scale)
```

```python
import functools
import math

import jax
import jax.numpy as jnp
from jax import lax
from jax.experimental import pallas as pl
from jax.experimental.pallas import tpu as pltpu
from jax.sharding import PartitionSpec as P

L = 64
MESH = pl.DeviceIdType.MESH
LANES = 128
ROWS = 16


def kernel(
    groups,
    spaces,
    slots_ref,
    momentum_ref,
    block_ref,
    out_ref,
    gathered,
    wide,
    left,
    weighted,
    part,
    part_in,
    rounded,
    rounded_in,
    local_sem,
    gather_send,
    gather_recv,
    pair_send,
    pair_recv,
    sum_send,
    sum_recv,
):
    block = block_ref.shape[1]
    site_count = block_ref.shape[2]
    total = groups * block
    rows = total // spaces
    planes = spaces // 2
    steps = block // 2
    span = 3 * site_count
    scale = jnp.float32(1.0 / math.sqrt(site_count * spaces))
    group = lax.axis_index("group")
    space = lax.axis_index("space")
    core = lax.rem(space, 2)
    plane = lax.div(space, 2)

    barrier = pltpu.get_barrier_semaphore()
    for off in range(1, groups):
        pl.semaphore_signal(
            barrier, inc=1, device_id={"group": lax.rem(group + off, groups)}, device_id_type=MESH
        )
    for off in range(1, planes):
        pl.semaphore_signal(
            barrier,
            inc=1,
            device_id={"space": lax.rem(plane + off, planes) * 2 + core},
            device_id_type=MESH,
        )
    pl.semaphore_signal(
        barrier, inc=1, device_id={"space": plane * 2 + 1 - core}, device_id_type=MESH
    )
    pl.semaphore_wait(barrier, groups + planes - 1)

    sends = []
    for off in range(1, groups):
        copy = pltpu.make_async_remote_copy(
            src_ref=block_ref,
            dst_ref=gathered.at[group],
            send_sem=gather_send.at[off - 1],
            recv_sem=gather_recv.at[off - 1],
            device_id={"group": lax.rem(group + off, groups)},
            device_id_type=MESH,
        )
        copy.start()
        sends.append(copy)
    own = pltpu.make_async_copy(block_ref, gathered.at[group], local_sem)
    own.start()

    sites = space * site_count + lax.broadcasted_iota(jnp.int32, (8, site_count), 1)
    coord_x = sites & (L - 1)
    coord_y = (sites >> 6) & (L - 1)
    coord_z = sites >> 12
    phase = momentum_ref[0] * coord_x + momentum_ref[1] * coord_y + momentum_ref[2] * coord_z
    angle = (phase & (L - 1)).astype(jnp.float32) * jnp.float32(2.0 * math.pi / L)
    cosine = jnp.cos(angle)[0:1]
    sine = jnp.sin(angle)[0:1]

    own.wait()
    for copy in sends:
        copy.wait()

    for q in range(groups):
        for c in range(6):
            wide[c, q * block : (q + 1) * block, :] = gathered[q, c].astype(jnp.float32)

    order = [(2 * z + h) * rows for h in range(2) for z in range(planes)]
    for a in range(3):
        real = wide[a]
        imag = wide[3 + a]
        first = [piece for i in order for piece in (real[i : i + rows], imag[i : i + rows])]
        second = [piece for i in order for piece in (-imag[i : i + rows], real[i : i + rows])]
        low, high = a * site_count, (a + 1) * site_count
        left[:, low:high] = jnp.concatenate(first, axis=0).astype(jnp.bfloat16)
        left[:, span + low : span + high] = jnp.concatenate(second, axis=0).astype(jnp.bfloat16)

    def fill(step):
        for half in range(2):
            k = slots_ref[group * block + 2 * step + half]
            row = [wide[c, pl.ds(k, 1), :] for c in range(6)]
            turn_re = [row[a] * cosine - row[3 + a] * sine for a in range(3)]
            turn_im = [row[a] * sine + row[3 + a] * cosine for a in range(3)]

            def tile(j, carry):
                top = pl.multiple_of(j * ROWS, ROWS)
                for s in range(0, site_count, LANES):
                    cols = slice(s, s + LANES)
                    re = [wide[a, pl.ds(top, ROWS), cols] for a in range(3)]
                    im = [wide[3 + a, pl.ds(top, ROWS), cols] for a in range(3)]
                    tr = [x[:, cols] for x in turn_re]
                    ti = [x[:, cols] for x in turn_im]
                    for a in range(3):
                        b, c = (a + 1) % 3, (a + 2) % 3
                        out_re = (re[b] * tr[c] - im[b] * ti[c]) - (re[c] * tr[b] - im[c] * ti[b])
                        out_im = (re[b] * ti[c] + im[b] * tr[c]) - (re[c] * ti[b] + im[c] * tr[b])
                        base = a * site_count + s
                        at = pl.ds(half * total + top, ROWS)
                        weighted[at, base : base + LANES] = out_re.astype(jnp.bfloat16)
                        weighted[at, span + base : span + base + LANES] = out_im.astype(jnp.bfloat16)
                return carry

            lax.fori_loop(0, total // ROWS, tile, 0, unroll=True)

    def pair_copy(step):
        return pltpu.make_async_remote_copy(
            src_ref=part.at[step, 1 - core],
            dst_ref=part_in.at[step],
            send_sem=pair_send.at[step],
            recv_sem=pair_recv.at[step],
            device_id={"space": plane * 2 + 1 - core},
            device_id_type=MESH,
        )

    def sum_copy(step, off):
        target = lax.rem(plane + off, planes)
        return pltpu.make_async_remote_copy(
            src_ref=rounded.at[step, target],
            dst_ref=rounded_in.at[off - 1, step],
            send_sem=sum_send.at[off - 1, step],
            recv_sem=sum_recv.at[off - 1, step],
            device_id={"space": target * 2 + core},
            device_id_type=MESH,
        )

    def forward(step):
        pair_copy(step).wait()
        rounded[step] = (part[step, core] + part_in[step]).astype(jnp.bfloat16)
        for off in range(1, planes):
            sum_copy(step, off).start()
        out_ref[pl.ds(2 * step, 2)] = part[step, core, plane] + part_in[step, plane]

    def body(step, carry):
        fill(step)
        product = lax.dot_general(
            left[...], weighted[...], (((1,), (1,)), ((), ())), preferred_element_type=jnp.float32
        )
        for half in range(2):
            piece = product[:, half * total : (half + 1) * total]
            part[step, :, :, half] = piece.reshape(2, planes, 2 * rows, total)
        pair_copy(step).start()

        @pl.when(step >= 1)
        def _():
            forward(step - 1)

        return carry

    lax.fori_loop(0, steps, body, 0)
    forward(steps - 1)

    def finish(step, carry):
        value = out_ref[pl.ds(2 * step, 2)]
        for off in range(1, planes):
            sum_copy(step, off).wait()
            value = value + rounded_in[off - 1, step].astype(jnp.float32)
        out_ref[pl.ds(2 * step, 2)] = value * scale
        return carry

    lax.fori_loop(0, steps, finish, 0)


def local(groups, spaces, vectors, momentum, assignment):
    block, _, _, site_count = vectors.shape
    total = block * groups
    rows = total // spaces
    planes = spaces // 2
    steps = block // 2
    mine = jnp.transpose(vectors, (1, 2, 0, 3)).reshape(6, block, site_count)
    dma = pltpu.SemaphoreType.DMA
    out = pl.pallas_call(
        functools.partial(kernel, groups, spaces),
        out_shape=jax.ShapeDtypeStruct((block, 2 * rows, total), jnp.float32),
        in_specs=[
            pl.BlockSpec(memory_space=pltpu.SMEM),
            pl.BlockSpec(memory_space=pltpu.SMEM),
            pl.BlockSpec(memory_space=pltpu.VMEM),
        ],
        out_specs=pl.BlockSpec(memory_space=pltpu.VMEM),
        scratch_shapes=[
            pltpu.VMEM((groups, 6, block, site_count), jnp.bfloat16),
            pltpu.VMEM((6, total, site_count), jnp.float32),
            pltpu.VMEM((2 * total, 6 * site_count), jnp.bfloat16),
            pltpu.VMEM((2 * total, 6 * site_count), jnp.bfloat16),
            pltpu.VMEM((steps, 2, planes, 2, 2 * rows, total), jnp.float32),
            pltpu.VMEM((steps, planes, 2, 2 * rows, total), jnp.float32),
            pltpu.VMEM((steps, planes, 2, 2 * rows, total), jnp.bfloat16),
            pltpu.VMEM((planes - 1, steps, 2, 2 * rows, total), jnp.bfloat16),
            dma,
            dma((groups - 1,)),
            dma((groups - 1,)),
            dma((steps,)),
            dma((steps,)),
            dma((planes - 1, steps)),
            dma((planes - 1, steps)),
        ],
        compiler_params=pltpu.CompilerParams(
            collective_id=0, has_side_effects=True, vmem_limit_bytes=48 * 1024 * 1024
        ),
    )(assignment, momentum, mine)
    return jnp.transpose(out.reshape(block, 2, rows, total), (2, 1, 0, 3))


def solution(mesh):
    return jax.shard_map(
        functools.partial(local, mesh.shape["group"], mesh.shape["space"]),
        mesh=mesh,
        in_specs=(P("group", None, None, "space"), P(), P()),
        out_specs=P("space", None, "group", None),
        check_vma=False,
    )
```

```python
import functools
import math

import jax
import jax.numpy as jnp
from jax import lax
from jax.experimental import pallas as pl
from jax.experimental.pallas import tpu as pltpu
from jax.sharding import PartitionSpec as P

L = 64
MESH = pl.DeviceIdType.MESH
LANES = 128
ROWS = 16
SLOTS = 4


def kernel(
    groups,
    spaces,
    slots_ref,
    momentum_ref,
    block_ref,
    out_ref,
    gathered,
    wide,
    right,
    weighted,
    part,
    part_in,
    rounded,
    rounded_in,
    local_sem,
    gather_send,
    gather_recv,
    pair_send,
    pair_recv,
    sum_send,
    sum_recv,
):
    block = block_ref.shape[1]
    site_count = block_ref.shape[2]
    total = groups * block
    rows = total // spaces
    planes = spaces // 2
    steps = block // SLOTS
    span = 3 * site_count
    scale = jnp.float32(1.0 / math.sqrt(site_count * spaces))
    group = lax.axis_index("group")
    space = lax.axis_index("space")
    core = lax.rem(space, 2)
    plane = lax.div(space, 2)

    barrier = pltpu.get_barrier_semaphore()
    for off in range(1, groups):
        pl.semaphore_signal(
            barrier, inc=1, device_id={"group": lax.rem(group + off, groups)}, device_id_type=MESH
        )
    for off in range(1, planes):
        pl.semaphore_signal(
            barrier,
            inc=1,
            device_id={"space": lax.rem(plane + off, planes) * 2 + core},
            device_id_type=MESH,
        )
    pl.semaphore_signal(
        barrier, inc=1, device_id={"space": plane * 2 + 1 - core}, device_id_type=MESH
    )
    pl.semaphore_wait(barrier, groups + planes - 1)

    def gather_copy(lane, target, source, owner, first, count):
        at = pl.ds(first, count)
        return pltpu.make_async_remote_copy(
            src_ref=source.at[at],
            dst_ref=gathered.at[owner, at],
            send_sem=gather_send.at[lane],
            recv_sem=gather_recv.at[lane],
            device_id={"group": target},
            device_id_type=MESH,
        )

    square = groups == 4
    if square:
        beside = group + 1 - 2 * lax.rem(group, 2)
        across = group + 2 - 4 * lax.div(group, 2)
        sends = [
            gather_copy(0, beside, block_ref, group, 0, 3),
            gather_copy(1, across, block_ref, group, 3, 3),
            gather_copy(2, beside, block_ref, group, 3, 3),
            gather_copy(3, across, block_ref, group, 0, 3),
        ]
        passed = [
            gather_copy(4, across, gathered.at[beside], beside, 0, 3),
            gather_copy(5, beside, gathered.at[across], across, 3, 3),
        ]
    else:
        sends = [
            gather_copy(off - 1, lax.rem(group + off, groups), block_ref, group, 0, 6)
            for off in range(1, groups)
        ]
    for copy in sends:
        copy.start()
    own = pltpu.make_async_copy(block_ref, gathered.at[group], local_sem)
    own.start()
    if square:
        for copy, onward in zip(sends, passed):
            copy.wait_recv()
            onward.start()

    sites = space * site_count + lax.broadcasted_iota(jnp.int32, (8, site_count), 1)
    coord_x = sites & (L - 1)
    coord_y = (sites >> 6) & (L - 1)
    coord_z = sites >> 12
    phase = momentum_ref[0] * coord_x + momentum_ref[1] * coord_y + momentum_ref[2] * coord_z
    angle = (phase & (L - 1)).astype(jnp.float32) * jnp.float32(2.0 * math.pi / L)
    cosine = jnp.cos(angle)[0:1]
    sine = jnp.sin(angle)[0:1]

    own.wait()
    if square:
        for copy in sends[:2]:
            copy.wait_send()
        for copy in sends[2:] + passed:
            copy.wait()
    else:
        for copy in sends:
            copy.wait()

    for q in range(groups):
        for c in range(6):
            wide[c, q * block : (q + 1) * block, :] = gathered[q, c].astype(jnp.float32)

    order = [(2 * z + h) * rows for h in range(2) for z in range(planes)]
    for a in range(3):
        real = wide[a]
        imag = wide[3 + a]
        first = [piece for i in order for piece in (real[i : i + rows], imag[i : i + rows])]
        second = [piece for i in order for piece in (-imag[i : i + rows], real[i : i + rows])]
        low, high = a * site_count, (a + 1) * site_count
        right[low:high] = jnp.concatenate(first, axis=0).T.astype(jnp.bfloat16)
        right[span + low : span + high] = jnp.concatenate(second, axis=0).T.astype(jnp.bfloat16)

    def fill(step):
        def one(half, carry):
            k = slots_ref[group * block + SLOTS * step + half]
            row = [wide[c, pl.ds(k, 1), :] for c in range(6)]
            turn_re = [row[a] * cosine - row[3 + a] * sine for a in range(3)]
            turn_im = [row[a] * sine + row[3 + a] * cosine for a in range(3)]

            def tile(j, inner):
                top = pl.multiple_of(j * ROWS, ROWS)
                for s in range(0, site_count, LANES):
                    cols = slice(s, s + LANES)
                    re = [wide[a, pl.ds(top, ROWS), cols] for a in range(3)]
                    im = [wide[3 + a, pl.ds(top, ROWS), cols] for a in range(3)]
                    tr = [x[:, cols] for x in turn_re]
                    ti = [x[:, cols] for x in turn_im]
                    for a in range(3):
                        b, c = (a + 1) % 3, (a + 2) % 3
                        out_re = (re[b] * tr[c] - im[b] * ti[c]) - (re[c] * tr[b] - im[c] * ti[b])
                        out_im = (re[b] * ti[c] + im[b] * tr[c]) - (re[c] * ti[b] + im[c] * tr[b])
                        base = a * site_count + s
                        at = pl.ds(pl.multiple_of(half * total + top, ROWS), ROWS)
                        weighted[at, base : base + LANES] = out_re.astype(jnp.bfloat16)
                        weighted[at, span + base : span + base + LANES] = out_im.astype(jnp.bfloat16)
                return inner

            return lax.fori_loop(0, total // ROWS, tile, carry, unroll=True)

        lax.fori_loop(0, SLOTS, one, 0)

    def pair_copy(step):
        return pltpu.make_async_remote_copy(
            src_ref=part.at[step, 1 - core],
            dst_ref=part_in.at[step],
            send_sem=pair_send.at[step],
            recv_sem=pair_recv.at[step],
            device_id={"space": plane * 2 + 1 - core},
            device_id_type=MESH,
        )

    def sum_copy(step, off):
        target = lax.rem(plane + off, planes)
        return pltpu.make_async_remote_copy(
            src_ref=rounded.at[step, target],
            dst_ref=rounded_in.at[off - 1, step],
            send_sem=sum_send.at[off - 1, step],
            recv_sem=sum_recv.at[off - 1, step],
            device_id={"space": target * 2 + core},
            device_id_type=MESH,
        )

    def forward(step):
        pair_copy(step).wait()
        rounded[step] = (part[step, core] + part_in[step]).astype(jnp.bfloat16)
        for off in range(1, planes):
            sum_copy(step, off).start()
        out_ref[pl.ds(SLOTS * step, SLOTS)] = part[step, core, plane] + part_in[step, plane]

    def body(step, carry):
        fill(step)
        product = jnp.dot(weighted[...], right[...], preferred_element_type=jnp.float32)
        for half in range(SLOTS):
            piece = product[half * total : (half + 1) * total].T
            part[step, :, :, half] = piece.reshape(2, planes, 2 * rows, total)
        pair_copy(step).start()

        @pl.when(step >= 1)
        def _():
            forward(step - 1)

        return carry

    lax.fori_loop(0, steps, body, 0)
    forward(steps - 1)

    def finish(step, carry):
        value = out_ref[pl.ds(SLOTS * step, SLOTS)]
        for off in range(1, planes):
            sum_copy(step, off).wait()
            value = value + rounded_in[off - 1, step].astype(jnp.float32)
        out_ref[pl.ds(SLOTS * step, SLOTS)] = value * scale
        return carry

    lax.fori_loop(0, steps, finish, 0)


def local(groups, spaces, vectors, momentum, assignment):
    block, _, _, site_count = vectors.shape
    total = block * groups
    rows = total // spaces
    planes = spaces // 2
    steps = block // SLOTS
    mine = jnp.transpose(vectors, (1, 2, 0, 3)).reshape(6, block, site_count)
    dma = pltpu.SemaphoreType.DMA
    out = pl.pallas_call(
        functools.partial(kernel, groups, spaces),
        out_shape=jax.ShapeDtypeStruct((block, 2 * rows, total), jnp.float32),
        in_specs=[
            pl.BlockSpec(memory_space=pltpu.SMEM),
            pl.BlockSpec(memory_space=pltpu.SMEM),
            pl.BlockSpec(memory_space=pltpu.VMEM),
        ],
        out_specs=pl.BlockSpec(memory_space=pltpu.VMEM),
        scratch_shapes=[
            pltpu.VMEM((groups, 6, block, site_count), jnp.bfloat16),
            pltpu.VMEM((6, total, site_count), jnp.float32),
            pltpu.VMEM((6 * site_count, 2 * total), jnp.bfloat16),
            pltpu.VMEM((SLOTS * total, 6 * site_count), jnp.bfloat16),
            pltpu.VMEM((steps, 2, planes, SLOTS, 2 * rows, total), jnp.float32),
            pltpu.VMEM((steps, planes, SLOTS, 2 * rows, total), jnp.float32),
            pltpu.VMEM((steps, planes, SLOTS, 2 * rows, total), jnp.bfloat16),
            pltpu.VMEM((planes - 1, steps, SLOTS, 2 * rows, total), jnp.bfloat16),
            dma,
            dma((max(groups - 1, 6),)),
            dma((max(groups - 1, 6),)),
            dma((steps,)),
            dma((steps,)),
            dma((planes - 1, steps)),
            dma((planes - 1, steps)),
        ],
        compiler_params=pltpu.CompilerParams(
            collective_id=0, has_side_effects=True, vmem_limit_bytes=48 * 1024 * 1024
        ),
    )(assignment, momentum, mine)
    return jnp.transpose(out.reshape(block, 2, rows, total), (2, 1, 0, 3))


def solution(mesh):
    return jax.shard_map(
        functools.partial(local, mesh.shape["group"], mesh.shape["space"]),
        mesh=mesh,
        in_specs=(P("group", None, None, "space"), P(), P()),
        out_specs=P("space", None, "group", None),
        check_vma=False,
    )
```

```python
import functools
import math

import jax
import jax.numpy as jnp
from jax import lax
from jax.experimental import pallas as pl
from jax.experimental.pallas import tpu as pltpu
from jax.sharding import PartitionSpec as P

L = 64
MESH = pl.DeviceIdType.MESH
LANES = 128
ROWS = 16
SLOTS = 4


def kernel(
    groups,
    spaces,
    slots_ref,
    momentum_ref,
    block_ref,
    out_ref,
    gathered,
    wide,
    right,
    weighted,
    part,
    part_in,
    rounded,
    rounded_in,
    local_sem,
    gather_send,
    gather_recv,
    pair_send,
    pair_recv,
    sum_send,
    sum_recv,
):
    block = block_ref.shape[1]
    site_count = block_ref.shape[2]
    total = groups * block
    rows = total // spaces
    planes = spaces // 2
    steps = block // SLOTS
    span = 3 * site_count
    scale = jnp.float32(1.0 / math.sqrt(site_count * spaces))
    group = lax.axis_index("group")
    space = lax.axis_index("space")
    core = lax.rem(space, 2)
    plane = lax.div(space, 2)

    barrier = pltpu.get_barrier_semaphore()
    for off in range(1, groups):
        pl.semaphore_signal(
            barrier, inc=1, device_id={"group": lax.rem(group + off, groups)}, device_id_type=MESH
        )
    for off in range(1, planes):
        pl.semaphore_signal(
            barrier,
            inc=1,
            device_id={"space": lax.rem(plane + off, planes) * 2 + core},
            device_id_type=MESH,
        )
    pl.semaphore_signal(
        barrier, inc=1, device_id={"space": plane * 2 + 1 - core}, device_id_type=MESH
    )
    pl.semaphore_wait(barrier, groups + planes - 1)

    def gather_copy(lane, target, source, owner, first, count):
        at = pl.ds(first, count)
        return pltpu.make_async_remote_copy(
            src_ref=source.at[at],
            dst_ref=gathered.at[owner, at],
            send_sem=gather_send.at[lane],
            recv_sem=gather_recv.at[lane],
            device_id={"group": target},
            device_id_type=MESH,
        )

    square = groups == 4
    if square:
        beside = group + 1 - 2 * lax.rem(group, 2)
        across = group + 2 - 4 * lax.div(group, 2)
        sends = [
            gather_copy(0, beside, block_ref, group, 0, 3),
            gather_copy(1, across, block_ref, group, 3, 3),
            gather_copy(2, beside, block_ref, group, 3, 3),
            gather_copy(3, across, block_ref, group, 0, 3),
        ]
        passed = [
            gather_copy(4, across, gathered.at[beside], beside, 0, 3),
            gather_copy(5, beside, gathered.at[across], across, 3, 3),
        ]
    else:
        sends = [
            gather_copy(off - 1, lax.rem(group + off, groups), block_ref, group, 0, 6)
            for off in range(1, groups)
        ]
    for copy in sends:
        copy.start()
    own = pltpu.make_async_copy(block_ref, gathered.at[group], local_sem)
    own.start()
    if square:
        for copy, onward in zip(sends, passed):
            copy.wait_recv()
            onward.start()

    sites = space * site_count + lax.broadcasted_iota(jnp.int32, (8, site_count), 1)
    coord_x = sites & (L - 1)
    coord_y = (sites >> 6) & (L - 1)
    coord_z = sites >> 12
    phase = momentum_ref[0] * coord_x + momentum_ref[1] * coord_y + momentum_ref[2] * coord_z
    angle = (phase & (L - 1)).astype(jnp.float32) * jnp.float32(2.0 * math.pi / L)
    cosine = jnp.cos(angle)[0:1]
    sine = jnp.sin(angle)[0:1]

    own.wait()
    if square:
        for copy in sends[:2]:
            copy.wait_send()
        for copy in sends[2:] + passed:
            copy.wait()
    else:
        for copy in sends:
            copy.wait()

    for q in range(groups):
        for c in range(6):
            wide[c, q * block : (q + 1) * block, :] = gathered[q, c].astype(jnp.float32)

    for a in range(3):
        real = wide[a].T.astype(jnp.bfloat16)
        imag = wide[3 + a].T.astype(jnp.bfloat16)
        low, high = a * site_count, (a + 1) * site_count
        right[low:high, :total] = real
        right[low:high, total:] = imag
        right[span + low : span + high, :total] = -imag
        right[span + low : span + high, total:] = real

    def fill(step):
        def one(half, carry):
            k = slots_ref[group * block + SLOTS * step + half]
            row = [wide[c, pl.ds(k, 1), :] for c in range(6)]
            turn_re = [row[a] * cosine - row[3 + a] * sine for a in range(3)]
            turn_im = [row[a] * sine + row[3 + a] * cosine for a in range(3)]

            def tile(j, inner):
                top = pl.multiple_of(j * ROWS, ROWS)
                for s in range(0, site_count, LANES):
                    cols = slice(s, s + LANES)
                    re = [wide[a, pl.ds(top, ROWS), cols] for a in range(3)]
                    im = [wide[3 + a, pl.ds(top, ROWS), cols] for a in range(3)]
                    tr = [x[:, cols] for x in turn_re]
                    ti = [x[:, cols] for x in turn_im]
                    for a in range(3):
                        b, c = (a + 1) % 3, (a + 2) % 3
                        out_re = (re[b] * tr[c] - im[b] * ti[c]) - (re[c] * tr[b] - im[c] * ti[b])
                        out_im = (re[b] * ti[c] + im[b] * tr[c]) - (re[c] * ti[b] + im[c] * tr[b])
                        base = a * site_count + s
                        at = pl.ds(pl.multiple_of(half * total + top, ROWS), ROWS)
                        weighted[at, base : base + LANES] = out_re.astype(jnp.bfloat16)
                        weighted[at, span + base : span + base + LANES] = out_im.astype(jnp.bfloat16)
                return inner

            return lax.fori_loop(0, total // ROWS, tile, carry, unroll=True)

        lax.fori_loop(0, SLOTS, one, 0)

    def pair_copy(step):
        return pltpu.make_async_remote_copy(
            src_ref=part.at[step, 1 - core],
            dst_ref=part_in.at[step],
            send_sem=pair_send.at[step],
            recv_sem=pair_recv.at[step],
            device_id={"space": plane * 2 + 1 - core},
            device_id_type=MESH,
        )

    def sum_copy(step, off):
        target = lax.rem(plane + off, planes)
        return pltpu.make_async_remote_copy(
            src_ref=rounded.at[step, target],
            dst_ref=rounded_in.at[off - 1, step],
            send_sem=sum_send.at[off - 1, step],
            recv_sem=sum_recv.at[off - 1, step],
            device_id={"space": target * 2 + core},
            device_id_type=MESH,
        )

    def forward(step):
        pair_copy(step).wait()
        rounded[step] = (part[step, core] + part_in[step]).astype(jnp.bfloat16)
        for off in range(1, planes):
            sum_copy(step, off).start()
        out_ref[pl.ds(SLOTS * step, SLOTS)] = part[step, core, plane] + part_in[step, plane]

    def body(step, carry):
        fill(step)

        @pl.when(step >= 1)
        def _():
            forward(step - 1)

        product = jnp.dot(weighted[...], right[...], preferred_element_type=jnp.float32)
        for half in range(SLOTS):
            piece = product[half * total : (half + 1) * total].T
            for c in range(2):
                for i in range(spaces):
                    first = c * total + i * rows
                    part[step, i % 2, i // 2, half, c * rows : (c + 1) * rows] = piece[
                        first : first + rows
                    ]
        pair_copy(step).start()

        return carry

    lax.fori_loop(0, steps, body, 0)
    forward(steps - 1)

    def finish(step, carry):
        value = out_ref[pl.ds(SLOTS * step, SLOTS)]
        for off in range(1, planes):
            sum_copy(step, off).wait()
            value = value + rounded_in[off - 1, step].astype(jnp.float32)
        out_ref[pl.ds(SLOTS * step, SLOTS)] = value * scale
        return carry

    lax.fori_loop(0, steps, finish, 0)


def local(groups, spaces, vectors, momentum, assignment):
    block, _, _, site_count = vectors.shape
    total = block * groups
    rows = total // spaces
    planes = spaces // 2
    steps = block // SLOTS
    mine = jnp.transpose(vectors, (1, 2, 0, 3)).reshape(6, block, site_count)
    dma = pltpu.SemaphoreType.DMA
    out = pl.pallas_call(
        functools.partial(kernel, groups, spaces),
        out_shape=jax.ShapeDtypeStruct((block, 2 * rows, total), jnp.float32),
        in_specs=[
            pl.BlockSpec(memory_space=pltpu.SMEM),
            pl.BlockSpec(memory_space=pltpu.SMEM),
            pl.BlockSpec(memory_space=pltpu.VMEM),
        ],
        out_specs=pl.BlockSpec(memory_space=pltpu.VMEM),
        scratch_shapes=[
            pltpu.VMEM((groups, 6, block, site_count), jnp.bfloat16),
            pltpu.VMEM((6, total, site_count), jnp.float32),
            pltpu.VMEM((6 * site_count, 2 * total), jnp.bfloat16),
            pltpu.VMEM((SLOTS * total, 6 * site_count), jnp.bfloat16),
            pltpu.VMEM((steps, 2, planes, SLOTS, 2 * rows, total), jnp.float32),
            pltpu.VMEM((steps, planes, SLOTS, 2 * rows, total), jnp.float32),
            pltpu.VMEM((steps, planes, SLOTS, 2 * rows, total), jnp.bfloat16),
            pltpu.VMEM((planes - 1, steps, SLOTS, 2 * rows, total), jnp.bfloat16),
            dma,
            dma((max(groups - 1, 6),)),
            dma((max(groups - 1, 6),)),
            dma((steps,)),
            dma((steps,)),
            dma((planes - 1, steps)),
            dma((planes - 1, steps)),
        ],
        compiler_params=pltpu.CompilerParams(
            collective_id=0, has_side_effects=True, vmem_limit_bytes=48 * 1024 * 1024
        ),
    )(assignment, momentum, mine)
    return jnp.transpose(out.reshape(block, 2, rows, total), (2, 1, 0, 3))


def solution(mesh):
    return jax.shard_map(
        functools.partial(local, mesh.shape["group"], mesh.shape["space"]),
        mesh=mesh,
        in_specs=(P("group", None, None, "space"), P(), P()),
        out_specs=P("space", None, "group", None),
        check_vma=False,
    )
```

```python
import functools
import math

import jax
import jax.numpy as jnp
from jax import lax
from jax.experimental import pallas as pl
from jax.experimental.pallas import tpu as pltpu
from jax.sharding import PartitionSpec as P

L = 64
MESH = pl.DeviceIdType.MESH
LANES = 128
ROWS = 16
SLOTS = 4


def kernel(
    groups,
    spaces,
    slots_ref,
    momentum_ref,
    block_ref,
    out_ref,
    gathered,
    wide,
    right,
    weighted,
    part,
    pair_out,
    part_in,
    rounded,
    rounded_in,
    local_sem,
    gather_send,
    gather_recv,
    pair_send,
    pair_recv,
    sum_send,
    sum_recv,
):
    block = block_ref.shape[1]
    site_count = block_ref.shape[2]
    total = groups * block
    rows = total // spaces
    planes = spaces // 2
    steps = block // SLOTS
    span = 3 * site_count
    scale = jnp.float32(1.0 / math.sqrt(site_count * spaces))
    group = lax.axis_index("group")
    space = lax.axis_index("space")
    core = lax.rem(space, 2)
    plane = lax.div(space, 2)

    barrier = pltpu.get_barrier_semaphore()
    for off in range(1, groups):
        pl.semaphore_signal(
            barrier, inc=1, device_id={"group": lax.rem(group + off, groups)}, device_id_type=MESH
        )
    for off in range(1, planes):
        pl.semaphore_signal(
            barrier,
            inc=1,
            device_id={"space": lax.rem(plane + off, planes) * 2 + core},
            device_id_type=MESH,
        )
    pl.semaphore_signal(
        barrier, inc=1, device_id={"space": plane * 2 + 1 - core}, device_id_type=MESH
    )
    pl.semaphore_wait(barrier, groups + planes - 1)

    def gather_copy(lane, target, source, owner, first, count):
        at = pl.ds(first, count)
        return pltpu.make_async_remote_copy(
            src_ref=source.at[at],
            dst_ref=gathered.at[owner, at],
            send_sem=gather_send.at[lane],
            recv_sem=gather_recv.at[lane],
            device_id={"group": target},
            device_id_type=MESH,
        )

    square = groups == 4
    if square:
        beside = group + 1 - 2 * lax.rem(group, 2)
        across = group + 2 - 4 * lax.div(group, 2)
        sends = [
            gather_copy(0, beside, block_ref, group, 0, 3),
            gather_copy(1, across, block_ref, group, 3, 3),
            gather_copy(2, beside, block_ref, group, 3, 3),
            gather_copy(3, across, block_ref, group, 0, 3),
        ]
        passed = [
            gather_copy(4, across, gathered.at[beside], beside, 0, 3),
            gather_copy(5, beside, gathered.at[across], across, 3, 3),
        ]
    else:
        sends = [
            gather_copy(off - 1, lax.rem(group + off, groups), block_ref, group, 0, 6)
            for off in range(1, groups)
        ]
    for copy in sends:
        copy.start()
    own = pltpu.make_async_copy(block_ref, gathered.at[group], local_sem)
    own.start()
    if square:
        for copy, onward in zip(sends, passed):
            copy.wait_recv()
            onward.start()

    sites = space * site_count + lax.broadcasted_iota(jnp.int32, (8, site_count), 1)
    coord_x = sites & (L - 1)
    coord_y = (sites >> 6) & (L - 1)
    coord_z = sites >> 12
    phase = momentum_ref[0] * coord_x + momentum_ref[1] * coord_y + momentum_ref[2] * coord_z
    angle = (phase & (L - 1)).astype(jnp.float32) * jnp.float32(2.0 * math.pi / L)
    cosine = jnp.cos(angle)[0:1]
    sine = jnp.sin(angle)[0:1]

    own.wait()
    if square:
        for copy in sends[:2]:
            copy.wait_send()
        for copy in sends[2:] + passed:
            copy.wait()
    else:
        for copy in sends:
            copy.wait()

    for q in range(groups):
        for c in range(6):
            wide[c, q * block : (q + 1) * block, :] = gathered[q, c].astype(jnp.float32)

    for a in range(3):
        real = wide[a].T.astype(jnp.bfloat16)
        imag = wide[3 + a].T.astype(jnp.bfloat16)
        low, high = a * site_count, (a + 1) * site_count
        right[low:high, :total] = real
        right[low:high, total:] = imag
        right[span + low : span + high, :total] = -imag
        right[span + low : span + high, total:] = real

    def fill(step, first, stop):
        def one(half, carry):
            k = slots_ref[group * block + SLOTS * step + half]
            row = [wide[c, pl.ds(k, 1), :] for c in range(6)]
            turn_re = [row[a] * cosine - row[3 + a] * sine for a in range(3)]
            turn_im = [row[a] * sine + row[3 + a] * cosine for a in range(3)]

            def tile(j, inner):
                top = pl.multiple_of(j * ROWS, ROWS)
                for s in range(0, site_count, LANES):
                    cols = slice(s, s + LANES)
                    re = [wide[a, pl.ds(top, ROWS), cols] for a in range(3)]
                    im = [wide[3 + a, pl.ds(top, ROWS), cols] for a in range(3)]
                    tr = [x[:, cols] for x in turn_re]
                    ti = [x[:, cols] for x in turn_im]
                    for a in range(3):
                        b, c = (a + 1) % 3, (a + 2) % 3
                        out_re = (re[b] * tr[c] - im[b] * ti[c]) - (re[c] * tr[b] - im[c] * ti[b])
                        out_im = (re[b] * ti[c] + im[b] * tr[c]) - (re[c] * ti[b] + im[c] * tr[b])
                        base = a * site_count + s
                        at = pl.ds(pl.multiple_of(half * total + top, ROWS), ROWS)
                        weighted[at, base : base + LANES] = out_re.astype(jnp.bfloat16)
                        weighted[at, span + base : span + base + LANES] = out_im.astype(jnp.bfloat16)
                return inner

            return lax.fori_loop(0, total // ROWS, tile, carry, unroll=True)

        lax.fori_loop(first, stop, one, 0)

    def pair_copy(step):
        return pltpu.make_async_remote_copy(
            src_ref=pair_out.at[step],
            dst_ref=part_in.at[step],
            send_sem=pair_send.at[step],
            recv_sem=pair_recv.at[step],
            device_id={"space": plane * 2 + 1 - core},
            device_id_type=MESH,
        )

    def sum_copy(step, off):
        target = lax.rem(plane + off, planes)
        return pltpu.make_async_remote_copy(
            src_ref=rounded.at[step, target],
            dst_ref=rounded_in.at[off - 1, step],
            send_sem=sum_send.at[off - 1, step],
            recv_sem=sum_recv.at[off - 1, step],
            device_id={"space": target * 2 + core},
            device_id_type=MESH,
        )

    def forward(step):
        pair_copy(step).wait()
        rounded[step] = (part[step, core] + part_in[step].astype(jnp.float32)).astype(jnp.bfloat16)
        for off in range(1, planes):
            sum_copy(step, off).start()
        out_ref[pl.ds(SLOTS * step, SLOTS)] = part[step, core, plane] + part_in[step, plane].astype(jnp.float32)

    def body(step, carry):
        fill(step, 0, SLOTS - 1)

        @pl.when(step >= 1)
        def _():
            forward(step - 1)

        fill(step, SLOTS - 1, SLOTS)
        product = jnp.dot(weighted[...], right[...], preferred_element_type=jnp.float32)
        for half in range(SLOTS):
            piece = product[half * total : (half + 1) * total].T
            for c in range(2):
                for i in range(spaces):
                    first = c * total + i * rows
                    part[step, i % 2, i // 2, half, c * rows : (c + 1) * rows] = piece[
                        first : first + rows
                    ]
        pair_out[step] = part[step, 1 - core].astype(jnp.bfloat16)
        pair_copy(step).start()

        return carry

    lax.fori_loop(0, steps, body, 0)
    forward(steps - 1)

    def finish(step, carry):
        value = out_ref[pl.ds(SLOTS * step, SLOTS)]
        for off in range(1, planes):
            sum_copy(step, off).wait()
            value = value + rounded_in[off - 1, step].astype(jnp.float32)
        out_ref[pl.ds(SLOTS * step, SLOTS)] = value * scale
        return carry

    lax.fori_loop(0, steps, finish, 0)


def local(groups, spaces, vectors, momentum, assignment):
    block, _, _, site_count = vectors.shape
    total = block * groups
    rows = total // spaces
    planes = spaces // 2
    steps = block // SLOTS
    mine = jnp.transpose(vectors, (1, 2, 0, 3)).reshape(6, block, site_count)
    dma = pltpu.SemaphoreType.DMA
    out = pl.pallas_call(
        functools.partial(kernel, groups, spaces),
        out_shape=jax.ShapeDtypeStruct((block, 2 * rows, total), jnp.float32),
        in_specs=[
            pl.BlockSpec(memory_space=pltpu.SMEM),
            pl.BlockSpec(memory_space=pltpu.SMEM),
            pl.BlockSpec(memory_space=pltpu.VMEM),
        ],
        out_specs=pl.BlockSpec(memory_space=pltpu.VMEM),
        scratch_shapes=[
            pltpu.VMEM((groups, 6, block, site_count), jnp.bfloat16),
            pltpu.VMEM((6, total, site_count), jnp.float32),
            pltpu.VMEM((6 * site_count, 2 * total), jnp.bfloat16),
            pltpu.VMEM((SLOTS * total, 6 * site_count), jnp.bfloat16),
            pltpu.VMEM((steps, 2, planes, SLOTS, 2 * rows, total), jnp.float32),
            pltpu.VMEM((steps, planes, SLOTS, 2 * rows, total), jnp.bfloat16),
            pltpu.VMEM((steps, planes, SLOTS, 2 * rows, total), jnp.bfloat16),
            pltpu.VMEM((steps, planes, SLOTS, 2 * rows, total), jnp.bfloat16),
            pltpu.VMEM((planes - 1, steps, SLOTS, 2 * rows, total), jnp.bfloat16),
            dma,
            dma((max(groups - 1, 6),)),
            dma((max(groups - 1, 6),)),
            dma((steps,)),
            dma((steps,)),
            dma((planes - 1, steps)),
            dma((planes - 1, steps)),
        ],
        compiler_params=pltpu.CompilerParams(
            collective_id=0, has_side_effects=True, vmem_limit_bytes=48 * 1024 * 1024
        ),
    )(assignment, momentum, mine)
    return jnp.transpose(out.reshape(block, 2, rows, total), (2, 1, 0, 3))


def solution(mesh):
    return jax.shard_map(
        functools.partial(local, mesh.shape["group"], mesh.shape["space"]),
        mesh=mesh,
        in_specs=(P("group", None, None, "space"), P(), P()),
        out_specs=P("space", None, "group", None),
        check_vma=False,
    )
```
